32 devices in a mesh: grp: 2 (over x), cuts: 16 (over z, y, core).
Axes of the slice: x: 2, y: 2, z: 4, core: 2. Of those that a mesh axis runs over, the one named last changes fastest.
Arguments:
- stem_tensor: bfloat16 [2, 128, 32, 512], P(None, ('grp', 'cuts')), parts along dimension 1
- branch_tensors: bfloat16 [2, 2, 2, 512, 512], replicated, may hold values from -0.1875 to 0.1875
- cut_values: int32 [128, 2], P(('grp', 'cuts')), parts along dimension 0, may hold values from 0 to 1
- bit_rows: int32 [16384], P('grp'), parts along dimension 0, may hold values from 0 to 31
- bit_cols: int32 [16384], P('grp'), parts along dimension 0, may hold values from 0 to 511
Outputs:
- amplitudes: float32 [2, 16384], P(None, ('grp', 'cuts')), parts along dimension 1
- log_scale: float32 [2], P('grp'), parts along dimension 0
The draws below stay inside these ranges and needn't reach their ends.
There are 2 independent parts, one for each index of `grp`. The reference program is written for one: setup_inputs(seed, part) draws one part's arguments, and reference() takes and returns one part's arrays. A program takes and returns all parts, laid end to end along the dimension named above; an argument that names none is the same for every part. Nothing has to cross between parts.
All inputs are finite; a program needn't handle non-finite values.
Results may differ from the reference program's by a relative error of at most 0.007.
Values sent between devices are 32-bit elements; how exact they have to be, the bound alone decides.
No kernel may reach another device: no remote copies, remote signals or barrier semaphores. Data moves between devices by JAX's collectives and lax.ppermute only.
A program may use at most 128 MiB of HBM per device.

```python
import jax
import jax.numpy as jnp
from jax import lax

K = 512
R = 32
STEPS = 2
SLICES = 64
NB = 8192


def draw_stem_tensor(key, part):
    first, second, third = jax.random.split(key, 3)
    order = jnp.arange(SLICES, dtype=jnp.float32)
    rising = jnp.exp(jnp.log(4.0) * order / max(SLICES - 1, 1))
    rough = jax.random.uniform(second, (SLICES,), jnp.float32, 0.6, 1.6)
    row_scale = jnp.exp(jax.random.uniform(third, (SLICES, R), jnp.float32, 0.0, jnp.log(10.0)))
    base = jax.random.normal(first, (2, SLICES, R, K), jnp.float32)
    values = base * (rising * rough)[None, :, None, None] * row_scale[None, :, :, None] / 4.0
    return values.astype(jnp.bfloat16)


def place_ends(array, rng, least, high):
    shape = array.shape
    spot = [jax.random.randint(jax.random.fold_in(rng, axis), (), 0, shape[axis]) for axis in range(len(shape))]
    array = array.at[tuple(spot)].set(least)
    longest = shape.index(max(shape))
    spot[longest] = (spot[longest] + 1) % shape[longest]
    return array.at[tuple(spot)].set(high)


def normal_values(rng, shape, width, reach, kind=jnp.bfloat16):
    result = jax.random.normal(rng, shape, jnp.float32) * width
    return jnp.minimum(jnp.maximum(result, -reach), reach).astype(kind)


def setup_inputs(seed: int = 0, part: int = 0) -> dict:
    key_list = jax.random.split(jax.random.key(seed), 6)
    part_splits = jax.random.split(jax.random.fold_in(key_list[5], part), 6)
    return {
        "stem_tensor": draw_stem_tensor(jax.random.fold_in(jax.random.fold_in(key_list[5], part), 71), part),
        "branch_tensors": normal_values(key_list[1], (STEPS, 2, 2, K, K), (2 * K) ** -0.5, 0.1875),
        "cut_values": place_ends(jax.random.randint(part_splits[2], (SLICES, STEPS), 0, 2), jax.random.fold_in(part_splits[2], 1), 0, 1).astype(jnp.int32),
        "bit_rows": place_ends(jax.random.randint(part_splits[3], (NB,), 0, R), jax.random.fold_in(part_splits[3], 1), 0, R - 1).astype(jnp.int32),
        "bit_cols": place_ends(jax.random.randint(part_splits[4], (NB,), 0, K), jax.random.fold_in(part_splits[4], 1), 0, K - 1).astype(jnp.int32),
    }


def reference(stem_tensor, branch_tensors, cut_values, bit_rows, bit_cols):
    state = jnp.moveaxis(stem_tensor, 1, 0)
    log_scale = jnp.zeros((1,), jnp.float32)
    table = jnp.zeros((2, R, K), jnp.float32)
    for step in range(STEPS):
        matrices = branch_tensors[step]

        def one_slice(pair):
            piece, value = pair
            chosen = lax.dynamic_index_in_dim(matrices, value, 0, keepdims=False)
            real_part = jnp.dot(piece[0], chosen[0], preferred_element_type=jnp.float32) - jnp.dot(piece[1], chosen[1], preferred_element_type=jnp.float32)
            imag_part = jnp.dot(piece[0], chosen[1], preferred_element_type=jnp.float32) + jnp.dot(piece[1], chosen[0], preferred_element_type=jnp.float32)
            return jnp.stack([real_part, imag_part])
        product = lax.map(one_slice, (state, cut_values[:, step]))
        peak = jnp.sqrt(jnp.max(product[:, 0] * product[:, 0] + product[:, 1] * product[:, 1])) + 1e-06
        log_scale = log_scale + jnp.log(peak)
        if step + 1 < STEPS:
            state = (product / peak).astype(jnp.bfloat16)
        else:
            table = lax.optimization_barrier(jnp.sum(product, axis=0)) / peak
    amplitudes = table[:, bit_rows, bit_cols]
    return (amplitudes, log_scale)
```

```python
import functools

import jax
import jax.numpy as jnp
from jax import lax
from jax.experimental import pallas as pl
from jax.experimental.pallas import tpu as pltpu
from jax.sharding import PartitionSpec as P

LANES = 128
TILE = 8


def fold(values, join):
    rows, columns = values.shape
    parts = [
        values[r : r + TILE, c : c + LANES]
        for r in range(0, rows, TILE)
        for c in range(0, columns, LANES)
    ]
    while len(parts) > 1:
        parts = [join(*parts[i : i + 2]) if i + 1 < len(parts) else parts[i] for i in range(0, len(parts), 2)]
    return parts[0]


def contract_kernel(cuts, stem, branch, out, held, weights, wide, stem_sem, branch_sem):
    _, slices, rows, width = held.shape
    steps = weights.shape[0]
    block = slices * rows
    stem_copy = pltpu.make_async_copy(stem, held, stem_sem)
    stem_copy.start()
    copies = {}
    for step in range(steps):
        for part in range(2):
            for value in range(2):
                copy = pltpu.make_async_copy(
                    branch.at[step, value, part],
                    weights.at[step, part, pl.ds(value * width, width)],
                    branch_sem.at[step, part, value],
                )
                copy.start()
                copies[step, part, value] = copy

    def place(step, part, piece, values):
        where = slice(part * block + piece * rows, part * block + (piece + 1) * rows)
        chosen = cuts[piece, step]
        start = pl.multiple_of(chosen * width, width)
        other = pl.multiple_of((1 - chosen) * width, width)
        wide[step, where, pl.ds(start, width)] = values
        wide[step, where, pl.ds(other, width)] = jnp.zeros_like(values)

    def product(step):
        result = []
        for part in range(2):
            for value in range(2):
                copies[step, part, value].wait()
            result.append(jnp.dot(wide[step], weights[step, part], preferred_element_type=jnp.float32))
        by_real, by_imag = result
        return by_real[:block] - by_imag[block:], by_imag[:block] + by_real[block:]

    stem_copy.wait()
    for part in range(2):
        for piece in range(slices):
            place(0, part, piece, held[part, piece])
    real_part, imag_part = product(0)
    for piece in range(slices):
        where = slice(piece * rows, (piece + 1) * rows)
        place(1, 0, piece, real_part[where].astype(jnp.bfloat16))
        place(1, 1, piece, imag_part[where].astype(jnp.bfloat16))
    square = fold(real_part * real_part + imag_part * imag_part, jnp.maximum)
    first = jnp.sqrt(jnp.max(square, axis=(0, 1), keepdims=True))
    scale = first + 1e-06
    inverse = 1.0 / scale
    real_part, imag_part = product(1)
    real_small = real_part * inverse
    imag_small = imag_part * inverse
    square = fold(real_small * real_small + imag_small * imag_small, jnp.maximum)
    second = jnp.sqrt(jnp.max(square, axis=(0, 1), keepdims=True)) * scale
    for part, whole in enumerate((real_part, imag_part)):
        total = whole[:rows]
        for piece in range(1, slices):
            total = total + whole[piece * rows : (piece + 1) * rows]
        for group in range(width // LANES):
            start = (group * 2 + part) * rows
            out[start : start + rows, :] = total[:, group * LANES : (group + 1) * LANES]
    index = lax.broadcasted_iota(jnp.int32, (TILE, LANES), 0)
    out[2 * rows * (width // LANES) :, :] = jnp.where(index == 0, first, second)


def contract(stem, branch, cuts):
    _, slices, rows, width = stem.shape
    steps = branch.shape[0]
    entries = 2 * rows * width // LANES
    return pl.pallas_call(
        contract_kernel,
        out_shape=jax.ShapeDtypeStruct((entries + TILE, LANES), jnp.float32),
        in_specs=[
            pl.BlockSpec(memory_space=pltpu.SMEM),
            pl.BlockSpec(memory_space=pl.ANY),
            pl.BlockSpec(memory_space=pl.ANY),
        ],
        out_specs=pl.BlockSpec(memory_space=pltpu.VMEM),
        scratch_shapes=[
            pltpu.VMEM(stem.shape, jnp.bfloat16),
            pltpu.VMEM((steps, 2, 2 * width, width), jnp.bfloat16),
            pltpu.VMEM((steps, 2 * slices * rows, 2 * width), jnp.bfloat16),
            pltpu.SemaphoreType.DMA,
            pltpu.SemaphoreType.DMA((steps, 2, 2)),
        ],
        cost_estimate=pl.CostEstimate(
            flops=steps * 16 * slices * rows * width * width, bytes_accessed=branch.size * 2, transcendentals=0
        ),
        name="contract",
    )(cuts, stem, branch)


def lookup_kernel(rows, chunks, place, own, got, bit_rows, bit_cols, out):
    entries = own.shape[0] - TILE
    groups = entries // (2 * rows)
    per_chunk = bit_rows.shape[0] // (2 * chunks * 2)
    table = own[:entries, :] + got[:entries, :]
    high = table.astype(jnp.bfloat16)
    low = (table - high.astype(jnp.float32)).astype(jnp.bfloat16)
    left = jnp.concatenate([high, low], axis=1)
    lane = lax.broadcasted_iota(jnp.int32, (LANES, LANES), 0)
    row = lax.broadcasted_iota(jnp.int32, (TILE, LANES), 0)

    def one(chunk, carry):
        first = (place[0] + chunk * place[1]) * per_chunk
        for group in range(per_chunk):
            wanted_col = bit_cols[pl.ds(first + group, 1), :]
            wanted_row = bit_rows[pl.ds(first + group, 1), :]
            hot = jnp.where(lane == (wanted_col & (LANES - 1)), 1.0, 0.0).astype(jnp.bfloat16)
            values = jnp.dot(left, jnp.concatenate([hot, hot], axis=0), preferred_element_type=jnp.float32)
            code = (wanted_col // LANES) * rows + wanted_row
            found = [jnp.zeros((TILE, LANES), jnp.float32) for _ in range(2)]
            for part_group in range(groups):
                for start in range(0, rows, TILE):
                    here = row + (part_group * rows + start) == code
                    for part in range(2):
                        begin = (part_group * 2 + part) * rows + start
                        found[part] = found[part] + jnp.where(here, values[begin : begin + TILE], 0.0)
            for part in range(2):
                out[chunk, pl.ds(2 * group + part, 1), :] = jnp.sum(found[part], axis=0, keepdims=True)
        return carry

    for chunk in range(chunks):
        one(chunk, 0)
    out[chunks] = jnp.maximum(own[entries:, :], got[entries:, :])


def lookup(rows, chunks, place, own, got, bit_rows, bit_cols):
    vmem = pl.BlockSpec(memory_space=pltpu.VMEM)
    return pl.pallas_call(
        functools.partial(lookup_kernel, rows, chunks),
        out_shape=jax.ShapeDtypeStruct((chunks + 1, TILE, LANES), jnp.float32),
        in_specs=[pl.BlockSpec(memory_space=pltpu.SMEM), vmem, vmem, vmem, vmem],
        out_specs=vmem,
        cost_estimate=pl.CostEstimate(flops=chunks * 2 * 512 * 256 * 256, bytes_accessed=1 << 20, transcendentals=0),
        name="lookup",
    )(place, own, got, bit_rows, bit_cols)


def swap(value, bit):
    return lax.ppermute(value, "cuts", [(i, i ^ bit) for i in range(lax.axis_size("cuts"))])


def merge(kept, arrived):
    return jnp.concatenate([kept[:-1] + arrived[:-1], jnp.maximum(kept[-1:], arrived[-1:])])


def exchange(held, bit, radix):
    mine = (lax.axis_index("cuts") // bit) % radix
    share = (held.shape[0] - 1) // radix

    def of(index):
        return jnp.concatenate([lax.dynamic_slice_in_dim(held, index * share, share), held[-1:]])

    arrived = [swap(of(mine ^ other), bit * other) for other in range(radix - 1, 0, -1)]
    result = of(mine)
    for value in arrived:
        result = merge(result, value)
    return result


def shards(stem_tensor, branch_tensors, cut_values, bit_rows, bit_cols):
    rows, width = stem_tensor.shape[2:]
    devices = lax.axis_size("cuts")
    half = devices // 4
    own = contract(stem_tensor, branch_tensors, cut_values)
    got = swap(own, 1)
    me = lax.axis_index("cuts")
    core, side = me % 2, (me // 2) % 2
    row_lines = bit_rows.reshape(-1, LANES)
    col_lines = bit_cols.reshape(-1, LANES)

    def chosen(which):
        place = jnp.stack([2 * which + core, jnp.int32(4)]).astype(jnp.int32)
        return lookup(rows, half, place, own, got, row_lines, col_lines)

    arrived = swap(chosen(1 - side), 2)
    held = merge(chosen(side), arrived)
    bit = 4
    while bit < devices:
        radix = 4 if bit * 4 <= devices else 2
        held = exchange(held, bit, radix)
        bit *= radix
    first = held[1, 0, 0] + 1e-06
    second = held[1, 1, 0] / first + 1e-06
    chunk = held[0].reshape(-1, 2, LANES).transpose(1, 0, 2).reshape(2, -1)
    amplitudes = chunk / first / second
    log_scale = jnp.log(first) + jnp.log(second)
    return amplitudes, log_scale.reshape(1)


def solution(mesh):
    placed = (
        P(None, ("grp", "cuts"), None, None),
        P(),
        P(("grp", "cuts"), None),
        P("grp"),
        P("grp"),
    )
    return jax.shard_map(
        shards,
        mesh=mesh,
        in_specs=placed,
        out_specs=(P(None, ("grp", "cuts")), P("grp")),
        check_vma=False,
    )
```

```python
import functools

import jax
import jax.numpy as jnp
from jax import lax
from jax.experimental import pallas as pl
from jax.experimental.pallas import tpu as pltpu
from jax.sharding import PartitionSpec as P

LANES = 128
TILE = 8


def fold(values, join):
    rows, columns = values.shape
    parts = [
        values[r : r + TILE, c : c + LANES]
        for r in range(0, rows, TILE)
        for c in range(0, columns, LANES)
    ]
    while len(parts) > 1:
        parts = [join(*parts[i : i + 2]) if i + 1 < len(parts) else parts[i] for i in range(0, len(parts), 2)]
    return parts[0]


def contract_kernel(cuts_in, stem, branch, rows_in, cols_in, out, lane_of, line_of, cuts, held, weights, wide, wanted, sems, branch_sem):
    _, slices, rows, width = held.shape
    steps = weights.shape[0]
    block = slices * rows
    cuts_copy = pltpu.make_async_copy(cuts_in, cuts, sems.at[0])
    stem_copy = pltpu.make_async_copy(stem, held, sems.at[1])
    cuts_copy.start()
    stem_copy.start()
    copies = {}
    for step in range(steps):
        for part in range(2):
            for value in range(2):
                copy = pltpu.make_async_copy(
                    branch.at[step, value, part],
                    weights.at[step, part, pl.ds(value * width, width)],
                    branch_sem.at[step, part, value],
                )
                copy.start()
                copies[step, part, value] = copy
    rows_copy = pltpu.make_async_copy(rows_in, wanted.at[0], sems.at[2])
    cols_copy = pltpu.make_async_copy(cols_in, wanted.at[1], sems.at[3])
    rows_copy.start()
    cols_copy.start()
    cuts_copy.wait()
    stem_copy.wait()

    def place(step, part, piece, values):
        where = slice(part * block + piece * rows, part * block + (piece + 1) * rows)
        chosen = cuts[step, piece]
        start = pl.multiple_of(chosen * width, width)
        other = pl.multiple_of((1 - chosen) * width, width)
        wide[step, where, pl.ds(start, width)] = values
        wide[step, where, pl.ds(other, width)] = jnp.zeros_like(values)

    def product(step):
        result = []
        for part in range(2):
            for value in range(2):
                copies[step, part, value].wait()
            result.append(jnp.dot(wide[step], weights[step, part], preferred_element_type=jnp.float32))
        by_real, by_imag = result
        return by_real[:block] - by_imag[block:], by_imag[:block] + by_real[block:]

    for part in range(2):
        for piece in range(slices):
            place(0, part, piece, held[part, piece])
    real_part, imag_part = product(0)
    for piece in range(slices):
        where = slice(piece * rows, (piece + 1) * rows)
        place(1, 0, piece, real_part[where].astype(jnp.bfloat16))
        place(1, 1, piece, imag_part[where].astype(jnp.bfloat16))
    square = fold(real_part * real_part + imag_part * imag_part, jnp.maximum)
    first = jnp.sqrt(jnp.max(square, axis=(0, 1), keepdims=True))
    scale = first + 1e-06
    inverse = 1.0 / scale
    rows_copy.wait()
    cols_copy.wait()
    columns = wanted[1]
    lane_of[...] = columns % LANES
    line_of[...] = columns // LANES * rows + wanted[0]
    real_part, imag_part = product(1)
    real_small = real_part * inverse
    imag_small = imag_part * inverse
    square = fold(real_small * real_small + imag_small * imag_small, jnp.maximum)
    second = jnp.sqrt(jnp.max(square, axis=(0, 1), keepdims=True)) * scale
    for part, whole in enumerate((real_part, imag_part)):
        total = whole[:rows]
        for piece in range(1, slices):
            total = total + whole[piece * rows : (piece + 1) * rows]
        for group in range(width // LANES):
            start = (group * 2 + part) * rows
            out[start : start + rows, :] = total[:, group * LANES : (group + 1) * LANES]
    index = lax.broadcasted_iota(jnp.int32, (TILE, LANES), 0)
    out[2 * rows * (width // LANES) :, :] = jnp.where(index == 0, first, second)


def in_hbm(value):
    return pltpu.with_memory_space_constraint(value, pltpu.HBM)


def in_vmem(value):
    return pltpu.with_memory_space_constraint(value, pltpu.VMEM)


def contract(stem, branch, cuts, bit_rows, bit_cols):
    _, slices, rows, width = stem.shape
    steps = branch.shape[0]
    entries = 2 * rows * width // LANES
    return pl.pallas_call(
        contract_kernel,
        out_shape=(
            pltpu.VMEM((entries + TILE, LANES), jnp.float32),
            pltpu.VMEM(bit_rows.shape, jnp.int32),
            pltpu.VMEM(bit_rows.shape, jnp.int32),
        ),
        in_specs=[pl.BlockSpec(memory_space=pl.ANY)] * 5,
        out_specs=[pl.BlockSpec(memory_space=pltpu.VMEM)] * 3,
        scratch_shapes=[
            pltpu.SMEM((steps, slices), jnp.int32),
            pltpu.VMEM(stem.shape, jnp.bfloat16),
            pltpu.VMEM((steps, 2, 2 * width, width), jnp.bfloat16),
            pltpu.VMEM((steps, 2 * slices * rows, 2 * width), jnp.bfloat16),
            pltpu.VMEM((2, *bit_rows.shape), jnp.int32),
            pltpu.SemaphoreType.DMA((4,)),
            pltpu.SemaphoreType.DMA((steps, 2, 2)),
        ],
        compiler_params=pltpu.CompilerParams(vmem_limit_bytes=32 << 20),
        cost_estimate=pl.CostEstimate(
            flops=steps * 16 * slices * rows * width * width, bytes_accessed=branch.size * 2, transcendentals=0
        ),
        name="contract",
    )(in_hbm(cuts.T), in_hbm(stem), in_hbm(branch), in_hbm(bit_rows), in_hbm(bit_cols))


def lookup_kernel(rows, chunks, other, own, got, lane_of, line_of, out):
    entries = own.shape[0] - TILE
    groups = entries // (2 * rows)
    per_chunk = lane_of.shape[0] // (2 * chunks * 2)
    me = lax.axis_index("cuts")
    side = (me // 2) % 2
    which = 2 * (1 - side if other else side) + me % 2
    table = own[:entries, :] + got[:entries, :]
    high = table.astype(jnp.bfloat16)
    low = (table - high.astype(jnp.float32)).astype(jnp.bfloat16)
    left = jnp.concatenate([high, low], axis=1)
    lane = lax.broadcasted_iota(jnp.int32, (LANES, LANES), 0)
    row = lax.broadcasted_iota(jnp.int32, (TILE, LANES), 0)

    def hot(line):
        return jnp.where(lane == lane_of[pl.ds(line, 1), :], 1.0, 0.0).astype(jnp.bfloat16)

    for chunk in range(chunks):
        first = (which + 4 * chunk) * per_chunk
        for pair in range(0, per_chunk, 2):
            right = jnp.concatenate([hot(first + pair), hot(first + pair + 1)], axis=1)
            both = jnp.dot(left, jnp.concatenate([right, right], axis=0), preferred_element_type=jnp.float32)
            for group in range(2):
                values = both[:, group * LANES : (group + 1) * LANES]
                wanted = line_of[pl.ds(first + pair + group, 1), :]
                found = [jnp.zeros((TILE, LANES), jnp.float32) for _ in range(2)]
                for part_group in range(groups):
                    for start in range(0, rows, TILE):
                        here = row + (part_group * rows + start) == wanted
                        for part in range(2):
                            begin = (part_group * 2 + part) * rows + start
                            found[part] = found[part] + jnp.where(here, values[begin : begin + TILE], 0.0)
                for part in range(2):
                    out[chunk, pl.ds(2 * (pair + group) + part, 1), :] = jnp.sum(found[part], axis=0, keepdims=True)
    out[chunks] = jnp.maximum(own[entries:, :], got[entries:, :])


def lookup(rows, chunks, other, *operands):
    vmem = pl.BlockSpec(memory_space=pltpu.VMEM)
    return pl.pallas_call(
        functools.partial(lookup_kernel, rows, chunks, other),
        out_shape=pltpu.VMEM((chunks + 1, TILE, LANES), jnp.float32),
        in_specs=[vmem] * 4,
        out_specs=vmem,
        compiler_params=pltpu.CompilerParams(vmem_limit_bytes=16 << 20),
        cost_estimate=pl.CostEstimate(flops=chunks * 2 * 512 * 256 * 256, bytes_accessed=1 << 20, transcendentals=0),
        name="lookup",
    )(*map(in_vmem, operands))


def finish_kernel(own, *rest):
    *arrived, amplitudes, log_scale = rest
    total = own[0]
    peaks = own[1]
    for value in arrived:
        total = total + value[0]
        peaks = jnp.maximum(peaks, value[1])
    first = peaks[0:1] + 1e-06
    second = peaks[1:2] / first + 1e-06
    total = total / first / second
    for group in range(TILE // 2):
        amplitudes[:, group * LANES : (group + 1) * LANES] = total[2 * group : 2 * group + 2]
    log_scale[...] = (jnp.log(first) + jnp.log(second))[:, :1]


def finish(*held):
    vmem = pl.BlockSpec(memory_space=pltpu.VMEM)
    amplitudes, log_scale = pl.pallas_call(
        finish_kernel,
        out_shape=(
            jax.ShapeDtypeStruct((2, TILE // 2 * LANES), jnp.float32),
            jax.ShapeDtypeStruct((1, 1), jnp.float32),
        ),
        in_specs=[vmem] * len(held),
        out_specs=[vmem] * 2,
        compiler_params=pltpu.CompilerParams(vmem_limit_bytes=1 << 20),
        name="finish",
    )(*map(in_vmem, held))
    return amplitudes, log_scale.reshape(1)


def swap(value, bit):
    return lax.ppermute(value, "cuts", [(i, i ^ bit) for i in range(lax.axis_size("cuts"))])


def merge(kept, arrived):
    return jnp.concatenate([kept[:-1] + arrived[:-1], jnp.maximum(kept[-1:], arrived[-1:])])


def exchange(held, bit, radix):
    mine = (lax.axis_index("cuts") // bit) % radix
    share = (held.shape[0] - 1) // radix

    def of(index):
        return jnp.concatenate([lax.dynamic_slice_in_dim(held, index * share, share), held[-1:]])

    arrived = [swap(of(mine ^ other), bit * other) for other in range(radix - 1, 0, -1)]
    return [of(mine), *arrived]


def shards(stem_tensor, branch_tensors, cut_values, bit_rows, bit_cols):
    rows, width = stem_tensor.shape[2:]
    devices = lax.axis_size("cuts")
    half = devices // 4
    own, lane_of, line_of = contract(
        stem_tensor, branch_tensors, cut_values, bit_rows.reshape(-1, LANES), bit_cols.reshape(-1, LANES)
    )
    got = swap(own, 1)
    arrived = swap(lookup(rows, half, True, own, got, lane_of, line_of), 2)
    pieces = [lookup(rows, half, False, own, got, lane_of, line_of), arrived]
    bit = 4
    while bit < devices:
        radix = 4 if bit * 4 <= devices else 2
        pieces = exchange(functools.reduce(merge, pieces), bit, radix)
        bit *= radix
    return finish(*pieces)


def solution(mesh):
    placed = (
        P(None, ("grp", "cuts"), None, None),
        P(),
        P(("grp", "cuts"), None),
        P("grp"),
        P("grp"),
    )
    return jax.shard_map(
        shards,
        mesh=mesh,
        in_specs=placed,
        out_specs=(P(None, ("grp", "cuts")), P("grp")),
        check_vma=False,
    )
```

```python
import functools

import jax
import jax.numpy as jnp
from jax import lax
from jax.experimental import pallas as pl
from jax.experimental.pallas import tpu as pltpu
from jax.sharding import PartitionSpec as P

LANES = 128
TILE = 8
STAGES = [(9,), (3, 5)]


def fold(values, join):
    rows, columns = values.shape
    parts = [
        values[r : r + TILE, c : c + LANES]
        for r in range(0, rows, TILE)
        for c in range(0, columns, LANES)
    ]
    while len(parts) > 1:
        parts = [join(*parts[i : i + 2]) if i + 1 < len(parts) else parts[i] for i in range(0, len(parts), 2)]
    return parts[0]


def contract_kernel(cuts_in, stem, branch, rows_in, cols_in, out, lane_of, line_of, cuts, held, weights, wide, wanted, sems, branch_sem):
    _, slices, rows, width = held.shape
    steps = weights.shape[0]
    block = slices * rows
    cuts_copy = pltpu.make_async_copy(cuts_in, cuts, sems.at[0])
    stem_copy = pltpu.make_async_copy(stem, held, sems.at[1])
    cuts_copy.start()
    stem_copy.start()
    copies = {}
    for step in range(steps):
        for part in range(2):
            for value in range(2):
                copy = pltpu.make_async_copy(
                    branch.at[step, value, part],
                    weights.at[step, part, pl.ds(value * width, width)],
                    branch_sem.at[step, part, value],
                )
                copy.start()
                copies[step, part, value] = copy
    rows_copy = pltpu.make_async_copy(rows_in, wanted.at[0], sems.at[2])
    cols_copy = pltpu.make_async_copy(cols_in, wanted.at[1], sems.at[3])
    rows_copy.start()
    cols_copy.start()
    cuts_copy.wait()
    stem_copy.wait()

    def place(step, part, piece, values):
        where = slice(part * block + piece * rows, part * block + (piece + 1) * rows)
        chosen = cuts[step, piece]
        start = pl.multiple_of(chosen * width, width)
        other = pl.multiple_of((1 - chosen) * width, width)
        wide[step, where, pl.ds(start, width)] = values
        wide[step, where, pl.ds(other, width)] = jnp.zeros_like(values)

    def product(step):
        result = []
        for part in range(2):
            for value in range(2):
                copies[step, part, value].wait()
        for part in range(2):
            result.append(jnp.dot(wide[step], weights[step, part], preferred_element_type=jnp.float32))
        by_real, by_imag = result
        return by_real[:block] - by_imag[block:], by_imag[:block] + by_real[block:]

    for part in range(2):
        for piece in range(slices):
            place(0, part, piece, held[part, piece])
    real_part, imag_part = product(0)
    for piece in range(slices):
        where = slice(piece * rows, (piece + 1) * rows)
        place(1, 0, piece, real_part[where].astype(jnp.bfloat16))
        place(1, 1, piece, imag_part[where].astype(jnp.bfloat16))
    square = fold(real_part * real_part + imag_part * imag_part, jnp.maximum)
    first = jnp.sqrt(jnp.max(square, axis=(0, 1), keepdims=True))
    scale = first + 1e-06
    inverse = 1.0 / scale
    rows_copy.wait()
    cols_copy.wait()
    columns = wanted[1]
    lane_of[...] = columns % LANES
    line_of[...] = columns // LANES * rows + wanted[0]
    real_part, imag_part = product(1)
    real_small = real_part * inverse
    imag_small = imag_part * inverse
    square = fold(real_small * real_small + imag_small * imag_small, jnp.maximum)
    second = jnp.sqrt(jnp.max(square, axis=(0, 1), keepdims=True)) * scale
    for part, whole in enumerate((real_part, imag_part)):
        total = whole[:rows]
        for piece in range(1, slices):
            total = total + whole[piece * rows : (piece + 1) * rows]
        for group in range(width // LANES):
            start = (group * 2 + part) * rows
            out[start : start + rows, :] = total[:, group * LANES : (group + 1) * LANES]
    index = lax.broadcasted_iota(jnp.int32, (TILE, LANES), 0)
    out[2 * rows * (width // LANES) :, :] = jnp.where(index == 0, first, second)


def in_hbm(value):
    return pltpu.with_memory_space_constraint(value, pltpu.HBM)


def in_vmem(value):
    return pltpu.with_memory_space_constraint(value, pltpu.VMEM)


def contract(stem, branch, cuts, bit_rows, bit_cols):
    _, slices, rows, width = stem.shape
    steps = branch.shape[0]
    entries = 2 * rows * width // LANES
    return pl.pallas_call(
        contract_kernel,
        out_shape=(
            pltpu.VMEM((entries + TILE, LANES), jnp.float32),
            pltpu.VMEM(bit_rows.shape, jnp.int32),
            pltpu.VMEM(bit_rows.shape, jnp.int32),
        ),
        in_specs=[pl.BlockSpec(memory_space=pl.ANY)] * 5,
        out_specs=[pl.BlockSpec(memory_space=pltpu.VMEM)] * 3,
        scratch_shapes=[
            pltpu.SMEM((steps, slices), jnp.int32),
            pltpu.VMEM(stem.shape, jnp.bfloat16),
            pltpu.VMEM((steps, 2, 2 * width, width), jnp.bfloat16),
            pltpu.VMEM((steps, 2 * slices * rows, 2 * width), jnp.bfloat16),
            pltpu.VMEM((2, *bit_rows.shape), jnp.int32),
            pltpu.SemaphoreType.DMA((4,)),
            pltpu.SemaphoreType.DMA((steps, 2, 2)),
        ],
        compiler_params=pltpu.CompilerParams(vmem_limit_bytes=32 << 20),
        cost_estimate=pl.CostEstimate(
            flops=steps * 16 * slices * rows * width * width, bytes_accessed=branch.size * 2, transcendentals=0
        ),
        name="contract",
    )(in_hbm(cuts.T), in_hbm(stem), in_hbm(branch), in_hbm(bit_rows), in_hbm(bit_cols))


def lookup_kernel(rows, offsets, own, got, lane_of, line_of, out):
    entries = own.shape[0] - TILE
    groups = entries // (2 * rows)
    me = lax.axis_index("cuts")
    per_chunk = lane_of.shape[0] // lax.axis_size("cuts")
    table = own[:entries, :] + got[:entries, :]
    high = table.astype(jnp.bfloat16)
    rest = (table - high.astype(jnp.float32)).astype(jnp.bfloat16)
    left = jnp.concatenate([high, rest], axis=1)
    lane = lax.broadcasted_iota(jnp.int32, (LANES, LANES), 0)
    row = lax.broadcasted_iota(jnp.int32, (TILE, LANES), 0)

    def hot(line):
        return jnp.where(lane == lane_of[pl.ds(line, 1), :], 1.0, 0.0).astype(jnp.bfloat16)

    for chunk, offset in enumerate(offsets):
        first = (me ^ offset) * per_chunk
        for pair in range(0, per_chunk, 2):
            right = jnp.concatenate([hot(first + pair), hot(first + pair + 1)], axis=1)
            both = jnp.dot(left, jnp.concatenate([right, right], axis=0), preferred_element_type=jnp.float32)
            for group in range(2):
                values = both[:, group * LANES : (group + 1) * LANES]
                wanted = line_of[pl.ds(first + pair + group, 1), :]
                found = [jnp.zeros((TILE, LANES), jnp.float32) for _ in range(2)]
                for part_group in range(groups):
                    for start in range(0, rows, TILE):
                        here = row + (part_group * rows + start) == wanted
                        for part in range(2):
                            begin = (part_group * 2 + part) * rows + start
                            found[part] = found[part] + jnp.where(here, values[begin : begin + TILE], 0.0)
                for part in range(2):
                    out[chunk, pl.ds(2 * (pair + group) + part, 1), :] = jnp.sum(found[part], axis=0, keepdims=True)
    out[len(offsets)] = jnp.maximum(own[entries:, :], got[entries:, :])


def lookup(rows, offsets, *operands):
    vmem = pl.BlockSpec(memory_space=pltpu.VMEM)
    return pl.pallas_call(
        functools.partial(lookup_kernel, rows, offsets),
        out_shape=pltpu.VMEM((len(offsets) + 1, TILE, LANES), jnp.float32),
        in_specs=[vmem] * 4,
        out_specs=vmem,
        compiler_params=pltpu.CompilerParams(vmem_limit_bytes=16 << 20),
        cost_estimate=pl.CostEstimate(
            flops=len(offsets) * 2 * 512 * 256 * 256, bytes_accessed=1 << 20, transcendentals=0
        ),
        name="lookup",
    )(*map(in_vmem, operands))


def finish_kernel(own, *rest):
    *arrived, amplitudes, log_scale = rest
    total = own[0]
    peaks = own[1]
    for value in arrived:
        total = total + value[0]
        peaks = jnp.maximum(peaks, value[1])
    first = peaks[0:1] + 1e-06
    second = peaks[1:2] / first + 1e-06
    total = total / first / second
    for group in range(TILE // 2):
        amplitudes[:, group * LANES : (group + 1) * LANES] = total[2 * group : 2 * group + 2]
    log_scale[...] = (jnp.log(first) + jnp.log(second))[:, :1]


def finish(*held):
    vmem = pl.BlockSpec(memory_space=pltpu.VMEM)
    amplitudes, log_scale = pl.pallas_call(
        finish_kernel,
        out_shape=(
            jax.ShapeDtypeStruct((2, TILE // 2 * LANES), jnp.float32),
            jax.ShapeDtypeStruct((1, 1), jnp.float32),
        ),
        in_specs=[vmem] * len(held),
        out_specs=[vmem] * 2,
        compiler_params=pltpu.CompilerParams(vmem_limit_bytes=1 << 20),
        name="finish",
    )(*map(in_vmem, held))
    return amplitudes, log_scale.reshape(1)


def stages(devices):
    if devices == 16:
        return STAGES
    result, bit = [], 2
    while bit < devices:
        result.append((bit + 1,))
        bit *= 2
    return result


def span(steps):
    found = [0]
    for step in steps:
        found = found + [step ^ other for other in found]
    return found


def nested(plan):
    return [a ^ b for a in span(plan[0]) for b in nested(plan[1:])] if plan else [0]


def swap(value, step):
    return lax.ppermute(value, "cuts", [(i, i ^ step) for i in range(lax.axis_size("cuts"))])


def merge(kept, arrived):
    return jnp.concatenate([kept[:-1] + arrived[:-1], jnp.maximum(kept[-1:], arrived[-1:])])


def shards(stem_tensor, branch_tensors, cut_values, bit_rows, bit_cols):
    rows = stem_tensor.shape[2]
    own, lane_of, line_of = contract(
        stem_tensor, branch_tensors, cut_values, bit_rows.reshape(-1, LANES), bit_cols.reshape(-1, LANES)
    )
    got = swap(own, 1)
    plan = stages(lax.axis_size("cuts"))
    pieces = None
    for index, steps in enumerate(plan):
        later = nested(plan[index + 1 :])
        count = len(later)
        offsets = span(steps)
        if pieces is None:
            parts = [
                functools.partial(lookup, rows, [offset ^ other for other in later], own, got, lane_of, line_of)
                for offset in offsets
            ]
        else:
            held = functools.reduce(merge, pieces)
            parts = [
                functools.partial(lambda at, held: jnp.concatenate([held[at : at + count], held[-1:]]), n * count, held)
                for n in range(len(offsets))
            ]
        arrived = [swap(part(), offset) for part, offset in reversed(list(zip(parts, offsets))[1:])]
        pieces = [parts[0](), *arrived]
    return finish(*pieces)


def solution(mesh):
    placed = (
        P(None, ("grp", "cuts"), None, None),
        P(),
        P(("grp", "cuts"), None),
        P("grp"),
        P("grp"),
    )
    return jax.shard_map(
        shards,
        mesh=mesh,
        in_specs=placed,
        out_specs=(P(None, ("grp", "cuts")), P("grp")),
        check_vma=False,
    )
```

```python
import functools

import jax
import jax.numpy as jnp
from jax import lax
from jax.experimental import pallas as pl
from jax.experimental.pallas import tpu as pltpu
from jax.sharding import PartitionSpec as P


LANES = 128
TILE = 8
STAGES = [(9,), (3, 5)]


def fold(values, join):
    rows, columns = values.shape
    parts = [
        values[r : r + TILE, c : c + LANES]
        for r in range(0, rows, TILE)
        for c in range(0, columns, LANES)
    ]
    while len(parts) > 1:
        parts = [join(*parts[i : i + 2]) if i + 1 < len(parts) else parts[i] for i in range(0, len(parts), 2)]
    return parts[0]


def contract_kernel(cuts_in, stem, branch, rows_in, cols_in, out, lane_of, line_of, cuts, held, weights, wide, wanted, sems, branch_sem):
    _, slices, rows, width = held.shape
    steps = weights.shape[0]
    cuts_copy = pltpu.make_async_copy(cuts_in, cuts, sems.at[0])
    stem_copy = pltpu.make_async_copy(stem, held, sems.at[1])
    cuts_copy.start()
    stem_copy.start()
    copies = {}
    for step in range(steps):
        for part in range(2):
            for value in range(2):
                copy = pltpu.make_async_copy(
                    branch.at[step, value, part],
                    weights.at[step, part, pl.ds(value * width, width)],
                    branch_sem.at[step, part, value],
                )
                copy.start()
                copies[step, part, value] = copy
    rows_copy = pltpu.make_async_copy(rows_in, wanted.at[0], sems.at[2])
    cols_copy = pltpu.make_async_copy(cols_in, wanted.at[1], sems.at[3])
    rows_copy.start()
    cols_copy.start()
    cuts_copy.wait()
    stem_copy.wait()

    def place(step, part, piece, values):
        where = slice((piece * 2 + part) * rows, (piece * 2 + part + 1) * rows)
        chosen = cuts[step, piece]
        start = pl.multiple_of(chosen * width, width)
        other = pl.multiple_of((1 - chosen) * width, width)
        wide[step, where, pl.ds(start, width)] = values
        wide[step, where, pl.ds(other, width)] = jnp.zeros_like(values)

    def product(step):
        for part in range(2):
            for value in range(2):
                copies[step, part, value].wait()
        real_all, imag_all = [], []
        per = max(slices // 2, 1)
        for b in range(slices // per):
            lhs = wide[step, b * per * 2 * rows : (b + 1) * per * 2 * rows]
            by_real = jnp.dot(lhs, weights[step, 0], preferred_element_type=jnp.float32)
            by_imag = jnp.dot(lhs, weights[step, 1], preferred_element_type=jnp.float32)
            for piece in range(per):
                re, im = slice(piece * 2 * rows, (piece * 2 + 1) * rows), slice((piece * 2 + 1) * rows, (piece * 2 + 2) * rows)
                real_all.append(by_real[re] - by_imag[im])
                imag_all.append(by_imag[re] + by_real[im])
        return jnp.concatenate(real_all, axis=0), jnp.concatenate(imag_all, axis=0)

    for part in range(2):
        for piece in range(slices):
            place(0, part, piece, held[part, piece])
    real_part, imag_part = product(0)
    for piece in range(slices):
        where = slice(piece * rows, (piece + 1) * rows)
        place(1, 0, piece, real_part[where].astype(jnp.bfloat16))
        place(1, 1, piece, imag_part[where].astype(jnp.bfloat16))
    square = fold(real_part * real_part + imag_part * imag_part, jnp.maximum)
    first = jnp.sqrt(jnp.max(square, axis=(0, 1), keepdims=True))
    scale = first + 1e-06
    inverse = 1.0 / scale
    rows_copy.wait()
    cols_copy.wait()
    columns = wanted[1]
    lane_of[...] = columns % LANES
    line_of[...] = columns // LANES * rows + wanted[0]
    real_part, imag_part = product(1)
    real_small = real_part * inverse
    imag_small = imag_part * inverse
    square = fold(real_small * real_small + imag_small * imag_small, jnp.maximum)
    second = jnp.sqrt(jnp.maximum(square[: TILE // 2], square[TILE // 2 :])) * scale
    for part, whole in enumerate((real_part, imag_part)):
        total = whole[:rows]
        for piece in range(1, slices):
            total = total + whole[piece * rows : (piece + 1) * rows]
        for group in range(width // LANES):
            start = (group * 2 + part) * rows
            out[start : start + rows, :] = total[:, group * LANES : (group + 1) * LANES]
    end = 2 * rows * (width // LANES)
    out[end : end + TILE // 2, :] = jnp.broadcast_to(first, second.shape)
    out[end + TILE // 2 :, :] = second


def in_hbm(value):
    return pltpu.with_memory_space_constraint(value, pltpu.HBM)


def in_vmem(value):
    return pltpu.with_memory_space_constraint(value, pltpu.VMEM)


def contract(stem, branch, cuts, bit_rows, bit_cols):
    _, slices, rows, width = stem.shape
    steps = branch.shape[0]
    entries = 2 * rows * width // LANES
    return pl.pallas_call(
        contract_kernel,
        out_shape=(
            pltpu.VMEM((entries + TILE, LANES), jnp.float32),
            pltpu.VMEM(bit_rows.shape, jnp.int32),
            pltpu.VMEM(bit_rows.shape, jnp.int32),
        ),
        in_specs=[pl.BlockSpec(memory_space=pl.ANY)] * 5,
        out_specs=[pl.BlockSpec(memory_space=pltpu.VMEM)] * 3,
        scratch_shapes=[
            pltpu.SMEM((steps, slices), jnp.int32),
            pltpu.VMEM(stem.shape, jnp.bfloat16),
            pltpu.VMEM((steps, 2, 2 * width, width), jnp.bfloat16),
            pltpu.VMEM((steps, 2 * slices * rows, 2 * width), jnp.bfloat16),
            pltpu.VMEM((2, *bit_rows.shape), jnp.int32),
            pltpu.SemaphoreType.DMA((4,)),
            pltpu.SemaphoreType.DMA((steps, 2, 2)),
        ],
        compiler_params=pltpu.CompilerParams(vmem_limit_bytes=32 << 20),
        cost_estimate=pl.CostEstimate(
            flops=steps * 16 * slices * rows * width * width, bytes_accessed=branch.size * 2, transcendentals=0
        ),
        name="contract",
    )(in_hbm(cuts.T), in_hbm(stem), in_hbm(branch), in_hbm(bit_rows), in_hbm(bit_cols))


def mark_kernel(offsets, lane_of, line_of, hot, lines):
    me = lax.axis_index("cuts")
    lane = lax.broadcasted_iota(jnp.int32, (LANES, LANES), 0)
    per_chunk = lines.shape[1]
    for chunk, offset in enumerate(offsets):
        for line in range(per_chunk):
            at = pl.ds((me ^ offset) * per_chunk + line, 1)
            lines[chunk, pl.ds(line, 1), :] = line_of[at, :]
            hot[chunk, :, line * LANES : (line + 1) * LANES] = jnp.where(lane == lane_of[at, :], 1.0, 0.0).astype(
                jnp.bfloat16
            )


def mark(offsets, lane_of, line_of):
    vmem = pl.BlockSpec(memory_space=pltpu.VMEM)
    per_chunk = lane_of.shape[0] // lax.axis_size("cuts")
    return pl.pallas_call(
        functools.partial(mark_kernel, offsets),
        out_shape=(
            pltpu.VMEM((len(offsets), LANES, per_chunk * LANES), jnp.bfloat16),
            pltpu.VMEM((len(offsets), per_chunk, LANES), jnp.int32),
        ),
        in_specs=[vmem] * 2,
        out_specs=[vmem] * 2,
        compiler_params=pltpu.CompilerParams(vmem_limit_bytes=8 << 20),
        cost_estimate=pl.CostEstimate(flops=100_000_000, bytes_accessed=len(offsets) << 17, transcendentals=0),
        name="mark",
    )(in_vmem(lane_of), in_vmem(line_of))


def lookup_kernel(rows, at, own, got, hot, line_of, out):
    entries = own.shape[0] - TILE
    groups = entries // (2 * rows)
    chunks, per_chunk = out.shape[0] - 1, line_of.shape[1]
    table = own[:entries, :] + got[:entries, :]
    high = table.astype(jnp.bfloat16)
    rest = (table - high.astype(jnp.float32)).astype(jnp.bfloat16)
    left = jnp.concatenate([high, rest], axis=1)
    row = lax.broadcasted_iota(jnp.int32, (TILE, LANES), 0)
    for chunk in range(chunks):
        for pair in range(0, per_chunk, 2):
            right = hot[at + chunk, :, pair * LANES : (pair + 2) * LANES]
            both = jnp.dot(left, jnp.concatenate([right, right], axis=0), preferred_element_type=jnp.float32)
            for group in range(2):
                values = both[:, group * LANES : (group + 1) * LANES]
                wanted = line_of[at + chunk, pl.ds(pair + group, 1), :]
                found = [jnp.zeros((TILE, LANES), jnp.float32) for _ in range(2)]
                for part_group in range(groups):
                    for start in range(0, rows, TILE):
                        here = row + (part_group * rows + start) == wanted
                        for part in range(2):
                            begin = (part_group * 2 + part) * rows + start
                            found[part] = found[part] + jnp.where(here, values[begin : begin + TILE], 0.0)
                for part in range(2):
                    out[chunk, pl.ds(2 * (pair + group) + part, 1), :] = jnp.sum(found[part], axis=0, keepdims=True)
    peaks = jnp.maximum(own[entries:, :], got[entries:, :])
    second = jnp.max(jnp.where(row < TILE // 2, 0.0, peaks), axis=(0, 1), keepdims=True)
    out[chunks] = jnp.where(row < TILE // 2, peaks, second)


def lookup(rows, at, count, *operands):
    vmem = pl.BlockSpec(memory_space=pltpu.VMEM)
    return pl.pallas_call(
        functools.partial(lookup_kernel, rows, at),
        out_shape=pltpu.VMEM((count + 1, TILE, LANES), jnp.float32),
        in_specs=[vmem] * 4,
        out_specs=vmem,
        compiler_params=pltpu.CompilerParams(vmem_limit_bytes=16 << 20),
        cost_estimate=pl.CostEstimate(
            flops=count * 2 * 512 * 256 * 256, bytes_accessed=1 << 20, transcendentals=0
        ),
        name="lookup",
    )(*map(in_vmem, operands))


def finish_kernel(own, *rest):
    *arrived, amplitudes, log_scale = rest
    total = own[0]
    peaks = own[1]
    for value in arrived:
        total = total + value[0]
        peaks = jnp.maximum(peaks, value[1])
    first = peaks[0:1] + 1e-06
    second = peaks[TILE - 1 :] / first + 1e-06
    total = total / first / second
    for group in range(TILE // 2):
        amplitudes[:, group * LANES : (group + 1) * LANES] = total[2 * group : 2 * group + 2]
    log_scale[...] = (jnp.log(first) + jnp.log(second))[:, :1]


def finish(*held):
    vmem = pl.BlockSpec(memory_space=pltpu.VMEM)
    amplitudes, log_scale = pl.pallas_call(
        finish_kernel,
        out_shape=(
            jax.ShapeDtypeStruct((2, TILE // 2 * LANES), jnp.float32),
            jax.ShapeDtypeStruct((1, 1), jnp.float32),
        ),
        in_specs=[vmem] * len(held),
        out_specs=[vmem] * 2,
        compiler_params=pltpu.CompilerParams(vmem_limit_bytes=1 << 20),
        name="finish",
    )(*map(in_vmem, held))
    return amplitudes, log_scale.reshape(1)


def stages(devices):
    if devices == 16:
        return STAGES
    result, bit = [], 2
    while bit < devices:
        result.append((bit + 1,))
        bit *= 2
    return result


def span(steps):
    found = [0]
    for step in steps:
        found = found + [step ^ other for other in found]
    return found


def nested(plan):
    return [a ^ b for a in span(plan[0]) for b in nested(plan[1:])] if plan else [0]


def swap(value, step):
    return lax.ppermute(value, "cuts", [(i, i ^ step) for i in range(lax.axis_size("cuts"))])


def merge(kept, arrived):
    return jnp.concatenate([kept[:-1] + arrived[:-1], jnp.maximum(kept[-1:], arrived[-1:])])


def body(stem_tensor, branch_tensors, cut_values, bit_rows, bit_cols):
    rows = stem_tensor.shape[2]
    plan = stages(lax.axis_size("cuts"))
    own, lane_of, line_of = contract(
        stem_tensor, branch_tensors, cut_values, bit_rows.reshape(-1, LANES), bit_cols.reshape(-1, LANES)
    )
    got = swap(own, 1)
    hot, lines = mark(nested(plan), lane_of, line_of)
    pieces = None
    for index, steps in enumerate(plan):
        count = len(nested(plan[index + 1 :]))
        offsets = span(steps)
        if pieces is None:
            parts = [
                functools.partial(lookup, rows, n * count, count, own, got, hot, lines)
                for n in range(len(offsets))
            ]
        else:
            held = functools.reduce(merge, pieces)
            parts = [
                functools.partial(lambda at, held: jnp.concatenate([held[at : at + count], held[-1:]]), n * count, held)
                for n in range(len(offsets))
            ]
        arrived = [swap(part(), offset) for part, offset in reversed(list(zip(parts, offsets))[1:])]
        pieces = [parts[0](), *arrived]
    return finish(*pieces)


def solution(mesh):
    placed = (
        P(None, ("grp", "cuts"), None, None),
        P(),
        P(("grp", "cuts"), None),
        P("grp"),
        P("grp"),
    )
    return jax.shard_map(
        body,
        mesh=mesh,
        in_specs=placed,
        out_specs=(P(None, ("grp", "cuts")), P("grp")),
        check_vma=False,
    )
```

```python
import functools

import jax
import jax.numpy as jnp
from jax import lax
from jax.experimental import pallas as pl
from jax.experimental.pallas import tpu as pltpu
from jax.sharding import PartitionSpec as P


LANES = 128
TILE = 8
STAGES = [(9,), (3, 5)]


def fold(values, join):
    rows, columns = values.shape
    parts = [
        values[r : r + TILE, c : c + LANES]
        for r in range(0, rows, TILE)
        for c in range(0, columns, LANES)
    ]
    while len(parts) > 1:
        parts = [join(*parts[i : i + 2]) if i + 1 < len(parts) else parts[i] for i in range(0, len(parts), 2)]
    return parts[0]


def contract_kernel(cuts_in, stem, branch, rows_in, cols_in, out, lane_of, line_of, cuts, held, weights, wide, wanted, sems, branch_sem):
    _, slices, rows, width = held.shape
    steps = weights.shape[0]
    cuts_copy = pltpu.make_async_copy(cuts_in, cuts, sems.at[0])
    stem_copy = pltpu.make_async_copy(stem, held, sems.at[1])
    cuts_copy.start()
    stem_copy.start()
    copies = {}
    for step in range(steps):
        for part in range(2):
            for value in range(2):
                copy = pltpu.make_async_copy(
                    branch.at[step, value, part],
                    weights.at[step, part, pl.ds(value * width, width)],
                    branch_sem.at[step, part, value],
                )
                copies[step, part, value] = copy
                if step == 0:
                    copy.start()
    rows_copy = pltpu.make_async_copy(rows_in, wanted.at[0], sems.at[2])
    cols_copy = pltpu.make_async_copy(cols_in, wanted.at[1], sems.at[3])
    rows_copy.start()
    cols_copy.start()
    cuts_copy.wait()
    for step in range(1, steps):
        for part in range(2):
            for value in range(2):
                copies[step, part, value].start()
    stem_copy.wait()

    def place(step, part, piece, values):
        where = slice((piece * 2 + part) * rows, (piece * 2 + part + 1) * rows)
        chosen = cuts[step, piece]
        start = pl.multiple_of(chosen * width, width)
        other = pl.multiple_of((1 - chosen) * width, width)
        wide[step, where, pl.ds(start, width)] = values
        wide[step, where, pl.ds(other, width)] = jnp.zeros_like(values)

    def product(step):
        for part in range(2):
            for value in range(2):
                copies[step, part, value].wait()
        real_all, imag_all = [], []
        per = max(slices // 2, 1)
        for b in range(slices // per):
            lhs = wide[step, b * per * 2 * rows : (b + 1) * per * 2 * rows]
            by_real = jnp.dot(lhs, weights[step, 0], preferred_element_type=jnp.float32)
            by_imag = jnp.dot(lhs, weights[step, 1], preferred_element_type=jnp.float32)
            for piece in range(per):
                re, im = slice(piece * 2 * rows, (piece * 2 + 1) * rows), slice((piece * 2 + 1) * rows, (piece * 2 + 2) * rows)
                real_all.append(by_real[re] - by_imag[im])
                imag_all.append(by_imag[re] + by_real[im])
        return jnp.concatenate(real_all, axis=0), jnp.concatenate(imag_all, axis=0)

    for part in range(2):
        for piece in range(slices):
            place(0, part, piece, held[part, piece])
    real_part, imag_part = product(0)
    for piece in range(slices):
        where = slice(piece * rows, (piece + 1) * rows)
        place(1, 0, piece, real_part[where].astype(jnp.bfloat16))
        place(1, 1, piece, imag_part[where].astype(jnp.bfloat16))
    square = fold(real_part * real_part + imag_part * imag_part, jnp.maximum)
    first = jnp.sqrt(jnp.max(square, axis=(0, 1), keepdims=True))
    scale = first + 1e-06
    inverse = 1.0 / scale
    rows_copy.wait()
    cols_copy.wait()
    columns = wanted[1]
    lane_of[...] = columns % LANES
    line_of[...] = columns // LANES * rows + wanted[0]
    real_part, imag_part = product(1)
    real_small = real_part * inverse
    imag_small = imag_part * inverse
    square = fold(real_small * real_small + imag_small * imag_small, jnp.maximum)
    second = jnp.sqrt(jnp.maximum(square[: TILE // 2], square[TILE // 2 :])) * scale
    for part, whole in enumerate((real_part, imag_part)):
        total = whole[:rows]
        for piece in range(1, slices):
            total = total + whole[piece * rows : (piece + 1) * rows]
        for group in range(width // LANES):
            start = (group * 2 + part) * rows
            out[start : start + rows, :] = total[:, group * LANES : (group + 1) * LANES]
    end = 2 * rows * (width // LANES)
    out[end : end + TILE // 2, :] = jnp.broadcast_to(first, second.shape)
    out[end + TILE // 2 :, :] = second


def in_hbm(value):
    return pltpu.with_memory_space_constraint(value, pltpu.HBM)


def in_vmem(value):
    return pltpu.with_memory_space_constraint(value, pltpu.VMEM)


def contract(stem, branch, cuts, bit_rows, bit_cols):
    _, slices, rows, width = stem.shape
    steps = branch.shape[0]
    entries = 2 * rows * width // LANES
    return pl.pallas_call(
        contract_kernel,
        out_shape=(
            pltpu.VMEM((entries + TILE, LANES), jnp.float32),
            pltpu.VMEM(bit_rows.shape, jnp.int32),
            pltpu.VMEM(bit_rows.shape, jnp.int32),
        ),
        in_specs=[pl.BlockSpec(memory_space=pl.ANY)] * 5,
        out_specs=[pl.BlockSpec(memory_space=pltpu.VMEM)] * 3,
        scratch_shapes=[
            pltpu.SMEM((steps, slices), jnp.int32),
            pltpu.VMEM(stem.shape, jnp.bfloat16),
            pltpu.VMEM((steps, 2, 2 * width, width), jnp.bfloat16),
            pltpu.VMEM((steps, 2 * slices * rows, 2 * width), jnp.bfloat16),
            pltpu.VMEM((2, *bit_rows.shape), jnp.int32),
            pltpu.SemaphoreType.DMA((4,)),
            pltpu.SemaphoreType.DMA((steps, 2, 2)),
        ],
        compiler_params=pltpu.CompilerParams(vmem_limit_bytes=32 << 20),
        cost_estimate=pl.CostEstimate(
            flops=steps * 16 * slices * rows * width * width, bytes_accessed=branch.size * 2, transcendentals=0
        ),
        name="contract",
    )(in_hbm(cuts.T), in_hbm(stem), in_hbm(branch), in_hbm(bit_rows), in_hbm(bit_cols))


def mark_kernel(offsets, lane_of, line_of, hot, lines):
    me = lax.axis_index("cuts")
    lane = lax.broadcasted_iota(jnp.int32, (LANES, LANES), 0)
    per_chunk = lines.shape[1]
    for chunk, offset in enumerate(offsets):
        for line in range(per_chunk):
            at = pl.ds((me ^ offset) * per_chunk + line, 1)
            lines[chunk, pl.ds(line, 1), :] = line_of[at, :]
            hot[chunk, :, line * LANES : (line + 1) * LANES] = jnp.where(lane == lane_of[at, :], 1.0, 0.0).astype(
                jnp.bfloat16
            )


def mark(offsets, lane_of, line_of):
    vmem = pl.BlockSpec(memory_space=pltpu.VMEM)
    per_chunk = lane_of.shape[0] // lax.axis_size("cuts")
    return pl.pallas_call(
        functools.partial(mark_kernel, offsets),
        out_shape=(
            pltpu.VMEM((len(offsets), LANES, per_chunk * LANES), jnp.bfloat16),
            pltpu.VMEM((len(offsets), per_chunk, LANES), jnp.int32),
        ),
        in_specs=[vmem] * 2,
        out_specs=[vmem] * 2,
        compiler_params=pltpu.CompilerParams(vmem_limit_bytes=8 << 20),
        cost_estimate=pl.CostEstimate(flops=100_000_000, bytes_accessed=len(offsets) << 17, transcendentals=0),
        name="mark",
    )(in_vmem(lane_of), in_vmem(line_of))


def lookup_kernel(rows, at, own, got, hot, line_of, out):
    entries = own.shape[0] - TILE
    groups = entries // (2 * rows)
    chunks, per_chunk = out.shape[0] - 1, line_of.shape[1]
    table = own[:entries, :] + got[:entries, :]
    high = table.astype(jnp.bfloat16)
    rest = (table - high.astype(jnp.float32)).astype(jnp.bfloat16)
    left = jnp.concatenate([high, rest], axis=1)
    row = lax.broadcasted_iota(jnp.int32, (TILE, LANES), 0)
    for chunk in range(chunks):
        for pair in range(0, per_chunk, 2):
            right = hot[at + chunk, :, pair * LANES : (pair + 2) * LANES]
            both = jnp.dot(left, jnp.concatenate([right, right], axis=0), preferred_element_type=jnp.float32)
            for group in range(2):
                values = both[:, group * LANES : (group + 1) * LANES]
                wanted = line_of[at + chunk, pl.ds(pair + group, 1), :]
                found = [jnp.zeros((TILE, LANES), jnp.float32) for _ in range(2)]
                for part_group in range(groups):
                    for start in range(0, rows, TILE):
                        here = row + (part_group * rows + start) == wanted
                        for part in range(2):
                            begin = (part_group * 2 + part) * rows + start
                            found[part] = found[part] + jnp.where(here, values[begin : begin + TILE], 0.0)
                for part in range(2):
                    out[chunk, pl.ds(2 * (pair + group) + part, 1), :] = jnp.sum(found[part], axis=0, keepdims=True)
    peaks = jnp.maximum(own[entries:, :], got[entries:, :])
    second = jnp.max(jnp.where(row < TILE // 2, 0.0, peaks), axis=(0, 1), keepdims=True)
    out[chunks] = jnp.where(row < TILE // 2, peaks, second)


def lookup(rows, at, count, *operands):
    vmem = pl.BlockSpec(memory_space=pltpu.VMEM)
    return pl.pallas_call(
        functools.partial(lookup_kernel, rows, at),
        out_shape=pltpu.VMEM((count + 1, TILE, LANES), jnp.float32),
        in_specs=[vmem] * 4,
        out_specs=vmem,
        compiler_params=pltpu.CompilerParams(vmem_limit_bytes=16 << 20),
        cost_estimate=pl.CostEstimate(
            flops=count * 2 * 512 * 256 * 256, bytes_accessed=1 << 20, transcendentals=0
        ),
        name="lookup",
    )(*map(in_vmem, operands))


def finish_kernel(own, *rest):
    *arrived, amplitudes, log_scale = rest
    total = own[0]
    peaks = own[1]
    for value in arrived:
        total = total + value[0]
        peaks = jnp.maximum(peaks, value[1])
    first = peaks[0:1] + 1e-06
    second = peaks[TILE - 1 :] / first + 1e-06
    total = total / first / second
    for group in range(TILE // 2):
        amplitudes[:, group * LANES : (group + 1) * LANES] = total[2 * group : 2 * group + 2]
    log_scale[...] = (jnp.log(first) + jnp.log(second))[:, :1]


def finish(*held):
    vmem = pl.BlockSpec(memory_space=pltpu.VMEM)
    amplitudes, log_scale = pl.pallas_call(
        finish_kernel,
        out_shape=(
            jax.ShapeDtypeStruct((2, TILE // 2 * LANES), jnp.float32),
            jax.ShapeDtypeStruct((1, 1), jnp.float32),
        ),
        in_specs=[vmem] * len(held),
        out_specs=[vmem] * 2,
        compiler_params=pltpu.CompilerParams(vmem_limit_bytes=1 << 20),
        name="finish",
    )(*map(in_vmem, held))
    return amplitudes, log_scale.reshape(1)


def stages(devices):
    if devices == 16:
        return STAGES
    result, bit = [], 2
    while bit < devices:
        result.append((bit + 1,))
        bit *= 2
    return result


def span(steps):
    found = [0]
    for step in steps:
        found = found + [step ^ other for other in found]
    return found


def nested(plan):
    return [a ^ b for a in span(plan[0]) for b in nested(plan[1:])] if plan else [0]


def swap(value, step):
    return lax.ppermute(value, "cuts", [(i, i ^ step) for i in range(lax.axis_size("cuts"))])


def merge(kept, arrived):
    return jnp.concatenate([kept[:-1] + arrived[:-1], jnp.maximum(kept[-1:], arrived[-1:])])


def body(stem_tensor, branch_tensors, cut_values, bit_rows, bit_cols):
    rows = stem_tensor.shape[2]
    plan = stages(lax.axis_size("cuts"))
    own, lane_of, line_of = contract(
        stem_tensor, branch_tensors, cut_values, bit_rows.reshape(-1, LANES), bit_cols.reshape(-1, LANES)
    )
    got = swap(own, 1)
    hot, lines = mark(nested(plan), lane_of, line_of)
    pieces = None
    for index, steps in enumerate(plan):
        count = len(nested(plan[index + 1 :]))
        offsets = span(steps)
        if pieces is None:
            parts = [
                functools.partial(lookup, rows, n * count, count, own, got, hot, lines)
                for n in range(len(offsets))
            ]
        else:
            held = functools.reduce(merge, pieces)
            parts = [
                functools.partial(lambda at, held: jnp.concatenate([held[at : at + count], held[-1:]]), n * count, held)
                for n in range(len(offsets))
            ]
        arrived = [swap(part(), offset) for part, offset in reversed(list(zip(parts, offsets))[1:])]
        pieces = [parts[0](), *arrived]
    return finish(*pieces)


def solution(mesh):
    placed = (
        P(None, ("grp", "cuts"), None, None),
        P(),
        P(("grp", "cuts"), None),
        P("grp"),
        P("grp"),
    )
    return jax.shard_map(
        body,
        mesh=mesh,
        in_specs=placed,
        out_specs=(P(None, ("grp", "cuts")), P("grp")),
        check_vma=False,
    )
```
